32 devices in a mesh: gx: 4 (over y, x), gy: 4 (over z), ma: 2 (over core).
Axes of the slice: x: 2, y: 2, z: 4, core: 2. Of those that a mesh axis runs over, the one named last changes fastest.
Arguments:
- object_field: float32 [2, 2048, 1536], P(None, 'gx', 'gy'), may hold values from -6 to 6
- probe: float32 [2, 4, 256, 256], P(None, 'ma'), may hold values from -3 to 3
- offsets: int32 [4, 4, 6, 2], P('gx', 'gy'), may hold values from 0 to 511, as said below
- counts: int32 [4, 4], P('gx', 'gy'), may hold values from 1 to 6, as said below
- amplitude: float32 [4, 4, 6, 256, 256], P('gx', 'gy'), may hold values from 0.5 to 3
Outputs:
- object_grad: float32 [2, 2048, 1536], P(None, ('gx', 'ma'), 'gy')
- probe_grad: float32 [2, 4, 256, 256], P(None, 'ma')
The draws below stay inside these ranges and needn't reach their ends.
Inputs may be any that keep to these rules, and one draw needn't show every extreme that they name: A tile's offsets are below 512 for rows and below 384 for columns; no patch passes the object's last row or column. `counts`: every tile holds at least one live position; in each tile row, tiles v and v + 2 hold at most 8 live positions together; in every draw some tile holds exactly 6 and its partner exactly 2.
All inputs are finite; a program needn't handle non-finite values.
Results may differ from the reference program's by a relative error of at most 0.0003.
Values sent between devices are 32-bit elements; how exact they have to be, the bound alone decides.
A program may use at most 128 MiB of HBM per device.

```python
import jax
import jax.numpy as jnp
from jax import lax

PS = 256
MODES = 4
TR = 512
TC = 384
CAP = 6
BAL = 4
TILES_X = 4
TILES_Y = 4
OX = 2048
OY = 1536


def draw_offsets(key, part):
    keys = jax.random.split(key, 4)
    shape_all = (TILES_X, TILES_Y, CAP)
    tile_row = jnp.arange(TILES_X, dtype=jnp.int32)[:, None, None]
    tile_col = jnp.arange(TILES_Y, dtype=jnp.int32)[None, :, None]
    row_limit = jnp.where(tile_row == TILES_X - 1, TR - PS + 1, TR)
    col_limit = jnp.where(tile_col == TILES_Y - 1, TC - PS + 1, TC)
    row_any = jax.random.randint(keys[0], shape_all, 0, row_limit)
    col_any = jax.random.randint(keys[1], shape_all, 0, col_limit)
    row_near = jax.random.randint(keys[2], shape_all, jnp.maximum(row_limit - PS // 2, 0), row_limit)
    col_near = jax.random.randint(keys[3], shape_all, jnp.maximum(col_limit - PS // 2, 0), col_limit)
    slot_ids = jnp.arange(CAP, dtype=jnp.int32)[None, None, :]
    row_all = jnp.where(slot_ids == 0, row_near, row_any)
    col_all = jnp.where(slot_ids == 0, col_near, col_any)
    row_all = row_all.at[0, 0, 0].set(TR - 1).at[0, 0, 1].set(0)
    col_all = col_all.at[0, 0, 0].set(TC - 1).at[0, 0, 1].set(0)
    return jnp.stack([row_all, col_all], axis=-1).astype(jnp.int32)


def draw_counts(key, part):
    keys = jax.random.split(key, 5)
    half_axis = TILES_Y // 2
    first = jax.random.randint(keys[0], (TILES_X, half_axis), 1, CAP + 1)
    second_limit = jnp.minimum(CAP, 2 * BAL - first)
    second = jax.random.randint(keys[1], (TILES_X, half_axis), 1, second_limit + 1)
    flipped = jax.random.randint(keys[2], (TILES_X, half_axis), 0, 2) == 1
    lower = jnp.where(flipped, second, first)
    upper = jnp.where(flipped, first, second)
    chosen_row = jax.random.randint(keys[3], (), 0, TILES_X)
    chosen_pair = jax.random.randint(keys[4], (), 0, half_axis)
    grid_row = jnp.arange(TILES_X, dtype=jnp.int32)[:, None]
    grid_pair = jnp.arange(half_axis, dtype=jnp.int32)[None, :]
    chosen = (grid_row == chosen_row) & (grid_pair == chosen_pair)
    lower = jnp.where(chosen, CAP, lower)
    upper = jnp.where(chosen, 2 * BAL - CAP, upper)
    return jnp.concatenate([lower, upper], axis=1).astype(jnp.int32)


def block_scale(rng, shape, pieces, least, top_value):
    factor_of, own = 1.0, jax.random.fold_in(rng, 6)
    for position, shards_of in pieces:
        heights = jnp.exp(jax.random.uniform(jax.random.fold_in(own, position), (shards_of,), jnp.float32, least / len(pieces), top_value / len(pieces)))
        factor_of = factor_of * jnp.repeat(heights, shape[position] // shards_of).reshape([-1 if axis == position else 1 for axis in range(len(shape))])
    return factor_of


def centred(stream_key, shape, scale, reach, cuts=(), kind=jnp.bfloat16):
    drawn = scale * jax.random.normal(stream_key, shape, jnp.float32)
    if cuts:
        drawn = drawn * block_scale(stream_key, shape, cuts, -0.22, 0.18)
    return jnp.clip(drawn, -reach, reach).astype(kind)


def setup_inputs(seed: int = 0) -> dict:
    key_of = jax.random.split(jax.random.key(seed), 6)
    return {
        "object_field": centred(key_of[0], (2, OX, OY), 1.0, 6.0, ((1, 4), (2, 4)), jnp.float32),
        "probe": centred(key_of[1], (2, MODES, PS, PS), 0.5, 3.0, ((1, 2),), jnp.float32),
        "offsets": draw_offsets(jax.random.fold_in(key_of[5], 71), 0),
        "counts": draw_counts(jax.random.fold_in(key_of[5], 71), 0),
        "amplitude": jnp.clip(0.5 + 2.5 * jax.random.uniform(key_of[4], (TILES_X, TILES_Y, CAP, PS, PS), jnp.float32) ** block_scale(key_of[4], (TILES_X, TILES_Y, CAP, PS, PS), ((0, 4), (1, 4)), -0.2, 0.2), 0.5, 3.0),
    }


def reference(object_field, probe, offsets, counts, amplitude):
    modes_c = probe[0] + 1j * probe[1]
    tile_total = TILES_X * TILES_Y
    corner_all = offsets.reshape(tile_total, CAP, 2)
    count_all = counts.reshape(tile_total)
    measured_all = amplitude.reshape(tile_total, CAP, PS, PS)
    tile_ids = jnp.arange(tile_total, dtype=jnp.int32)
    zero_index = jnp.zeros((), jnp.int32)

    def tile_step(carry, inputs):
        grad_field, grad_probe = carry
        tile_id, corners, live_count, measured = inputs
        row_start = (tile_id // TILES_Y * TR + corners[:, 0]).astype(jnp.int32)
        col_start = (tile_id % TILES_Y * TC + corners[:, 1]).astype(jnp.int32)

        def take_one(row_first, col_first):
            return lax.dynamic_slice(object_field, (zero_index, row_first, col_first), (2, PS, PS))
        patches = jax.vmap(take_one)(row_start, col_start)
        patch_c = patches[:, 0] + 1j * patches[:, 1]
        exit_wave = modes_c[None] * patch_c[:, None]
        far = jnp.fft.fft2(exit_wave, norm='ortho')
        power = lax.optimization_barrier(jnp.sum(far.real * far.real + far.imag * far.imag, axis=1))
        live = (jnp.arange(CAP, dtype=jnp.int32) < live_count).astype(object_field.dtype)
        factor = live[:, None, None] * (1.0 - measured / jnp.sqrt(jnp.maximum(power, 0.25)))
        back = jnp.fft.ifft2(far * factor[:, None], norm='ortho')
        grad_probe = grad_probe + lax.optimization_barrier(jnp.sum(jnp.conj(patch_c)[:, None] * back, axis=0))
        patch_grad = lax.optimization_barrier(jnp.sum(jnp.conj(modes_c)[None] * back, axis=1))
        grad_parts = jnp.stack([patch_grad.real, patch_grad.imag], axis=1)

        def add_one(index_slot, accum):
            start = (zero_index, row_start[index_slot], col_start[index_slot])
            current = lax.dynamic_slice(accum, start, (2, PS, PS))
            return lax.dynamic_update_slice(accum, current + grad_parts[index_slot], start)
        grad_field = lax.fori_loop(0, CAP, add_one, grad_field)
        return ((grad_field, grad_probe), None)
    start_carry = (jnp.zeros_like(object_field), jnp.zeros(modes_c.shape, modes_c.dtype))
    final_carry, unused = lax.scan(tile_step, start_carry, (tile_ids, corner_all, count_all, measured_all))
    grad_field, grad_probe = final_carry
    return (grad_field, jnp.stack([grad_probe.real, grad_probe.imag]))
```

```python
import functools

import jax
import jax.numpy as jnp
import ml_dtypes
import numpy as np
from jax import lax
from jax.experimental import pallas as pl
from jax.experimental.pallas import tpu as pltpu
from jax.sharding import PartitionSpec as P

F32 = jnp.float32
BF16 = jnp.bfloat16
MESH = pl.DeviceIdType.MESH
ANY = pl.BlockSpec(memory_space=pl.ANY)
SM = pl.BlockSpec(memory_space=pltpu.SMEM)
VM = pl.BlockSpec(memory_space=pltpu.VMEM)


def tables(side):
    half = side // 2
    line = np.arange(half)
    found = []
    for odd in (0, 1):
        product = (2 * line[:, None] + odd) * line[None, :] % side
        value = np.exp(-2j * np.pi * product / side) / np.sqrt(side)
        block = np.block([[value.real, -value.imag], [value.imag, value.real]])
        found.append(block)

    def parts(block):
        high = block.astype(np.float32).astype(ml_dtypes.bfloat16)
        low = (block - high.astype(np.float64)).astype(np.float32).astype(ml_dtypes.bfloat16)
        return high, high, low

    tall = [np.concatenate(parts(b), 0) for b in (found[0].T, found[1].T, found[0], found[1])]
    wide = [np.concatenate(parts(b), 1) for b in (found[0], found[1], found[0].T, found[1].T)]
    order = np.concatenate([np.arange(0, side, 2), np.arange(1, side, 2)])
    pick = np.zeros((side, side), np.float32)
    pick[order, np.arange(side)] = 1.0
    picks = np.stack([pick, pick.T]).astype(ml_dtypes.bfloat16)
    return np.stack(tall), np.stack(wide), picks


def split(x):
    high = x.astype(BF16)
    return high, (x - high.astype(F32)).astype(BF16)


def right_mul(x, table):
    high, low = split(x)
    return jnp.dot(jnp.concatenate([high, low, high], 1), table, preferred_element_type=F32)


def left_mul(table, x):
    high, low = split(x)
    return jnp.dot(table, jnp.concatenate([high, low, high], 0), preferred_element_type=F32)


def remote(src, dst, send, recv, where):
    return pltpu.make_async_remote_copy(src_ref=src, dst_ref=dst, send_sem=send, recv_sem=recv,
                                        device_id=where, device_id_type=MESH)


def fused_kernel(nx, ny, off_ref, cnt_ref, obj, probe_hbm, amp_hbm, tall_hbm, wide_hbm, pick_hbm,
                 out, pout,
                 ext, probe, meas, tall, wide, pick, patch, far, pw, pwr, gp, gr, zbuf, grad,
                 acc, rg, rz, r_r, r_b, r_c, r_d, fin, lsem, hs, hr, ps, pr, gs, grs, es, er, as_, ar):
    u, v, m = lax.axis_index("gx"), lax.axis_index("gy"), lax.axis_index("ma")
    o = 1 - m
    side = probe.shape[2]
    half = side // 2
    pm = probe.shape[1]
    cap = meas.shape[0]
    rows, cols = obj.shape[1], obj.shape[2]
    other = (u, v, o)
    right, below = v < ny - 1, u < nx - 1
    left_dev, right_dev = (u, v - 1, m), (u, v + 1, m)
    up_dev, down_dev = (u - 1, v, m), (u + 1, v, m)

    local = [
        pltpu.make_async_copy(amp_hbm.at[0, 0], meas, lsem.at[0]),
        pltpu.make_async_copy(pick_hbm, pick, lsem.at[1]),
        pltpu.make_async_copy(obj, ext.at[:, 0:rows, 0:cols], lsem.at[2]),
        pltpu.make_async_copy(probe_hbm, probe, lsem.at[3]),
        pltpu.make_async_copy(tall_hbm, tall, lsem.at[4]),
        pltpu.make_async_copy(wide_hbm, wide, lsem.at[5]),
    ]
    for c in local:
        c.start()

    barrier = pltpu.get_barrier_semaphore()

    def greet(where):
        pl.semaphore_signal(barrier, inc=1, device_id=where, device_id_type=MESH)
    greet(other)
    for d in range(1, nx):
        greet((lax.rem(u + d, nx), v, m))
    for d in range(1, ny):
        greet((u, lax.rem(v + d, ny), m))

    @pl.when(jnp.logical_not(right))
    def _():
        ext[:, 0:rows, cols:cols + side] = jnp.zeros((2, rows, side), F32)

    @pl.when(jnp.logical_not(below))
    def _():
        ext[:, rows:rows + side, 0:cols] = jnp.zeros((2, side, cols), F32)

    @pl.when(jnp.logical_not(below & right))
    def _():
        ext[:, rows:rows + side, cols:cols + side] = jnp.zeros((2, side, side), F32)
    pl.semaphore_wait(barrier, nx + ny - 1)

    def piece(ref, r0, rn, c0, cn):
        return ref.at[m, r0:r0 + rn, c0:c0 + cn]

    h = rows - side
    first, rest = (0, side, cols, side), (side, h, cols, side)
    under, corner = (rows, side, 0, cols), (rows, side, cols, side)
    hops = [
        (piece(obj, 0, side, 0, side), first, v > 0, right, left_dev),
        (piece(obj, 0, side, 0, cols), under, u > 0, below, up_dev),
        (piece(obj, side, h, 0, side), rest, v > 0, right, left_dev),
        (piece(ext, *first), corner, (u > 0) & right, below & right, up_dev),
    ]
    outs, fwds = [], []
    for n, (src, place, goes, comes, target) in enumerate(hops):
        outs.append(remote(src, piece(ext, *place), hs.at[n], hr.at[n], target))
        fwds.append(remote(piece(ext, *place), piece(ext, *place), hs.at[4 + n], hr.at[4 + n], other))
    for n in range(3):
        @pl.when(hops[n][2])
        def _(n=n):
            outs[n].start()

    @pl.loop(0, zbuf.shape[0] // 8)
    def _(i):
        zbuf[pl.ds(pl.multiple_of(i * 8, 8), 8), :] = jnp.zeros((8, zbuf.shape[1]), F32)
    grad[...] = jnp.zeros_like(grad)
    acc[...] = jnp.zeros_like(acc)
    local[0].wait()
    local[1].wait()

    @pl.loop(0, cap)
    def _(s):
        measured = jnp.zeros((side, side), F32)
        for term in split(meas[s]):
            moved = jnp.dot(term, pick[0], preferred_element_type=F32).astype(BF16)
            measured = measured + jnp.dot(pick[1], moved, preferred_element_type=F32)
        meas[s] = measured

    for n, (src, place, goes, comes, target) in enumerate(hops):
        @pl.when(comes)
        def _(n=n):
            outs[n].wait_recv()
            if n == 0:
                @pl.when(u > 0)
                def _():
                    outs[3].start()
            fwds[n].start()
    for c in local[2:]:
        c.wait()
    for n, (src, place, goes, comes, target) in enumerate(hops):
        @pl.when(comes)
        def _(n=n):
            fwds[n].wait_recv()

    tall_rows, wide_cols = side + 8, side + 128

    def corner_of(s):
        row, col = off_ref[0, s], off_ref[1, s]
        return lax.rem(row, 8), lax.div(row, 8), lax.rem(col, 128), lax.div(col, 128)

    def bit_of(x, b):
        return lax.rem(x // b, 2) == 1

    def swap_power(s):
        return remote(pw.at[s], pwr.at[s], ps.at[s], pr.at[s], other)

    @pl.loop(0, cap)
    def _(s):
        drop, top, shift, base = corner_of(s)
        source = lax.broadcasted_iota(jnp.int32, (wide_cols, side), 0)
        place = lax.broadcasted_iota(jnp.int32, (wide_cols, side), 1)
        move = jnp.where(source == place + shift, 1.0, 0.0).astype(BF16)
        move = jnp.concatenate([move, move], 0)

        def take(part):
            x = ext[part, pl.ds(top * 8, tall_rows), pl.ds(base * 128, wide_cols)]
            x = jnp.dot(jnp.concatenate(split(x), 1), move, preferred_element_type=F32)
            for b in (4, 2, 1):
                x = jnp.where(bit_of(drop, b), pltpu.roll(x, tall_rows - b, 0), x)
            return x[:side]

        a_re, a_im = take(0), take(1)
        patch[s, 0] = a_re
        patch[s, 1] = a_im
        pow_e = pow_o = jnp.zeros((half, side), F32)
        for k in range(pm):
            p_re, p_im = probe[0, k], probe[1, k]
            e_re = p_re * a_re - p_im * a_im
            e_im = p_re * a_im + p_im * a_re
            x_e = jnp.concatenate([e_re[:, :half] + e_re[:, half:], e_im[:, :half] + e_im[:, half:]], 1)
            x_o = jnp.concatenate([e_re[:, :half] - e_re[:, half:], e_im[:, :half] - e_im[:, half:]], 1)
            z_e = right_mul(x_e, tall[0])
            z_o = right_mul(x_o, tall[1])
            z_re = jnp.concatenate([z_e[:, :half], z_o[:, :half]], 1)
            z_im = jnp.concatenate([z_e[:, half:], z_o[:, half:]], 1)
            y_e = jnp.concatenate([z_re[:half] + z_re[half:], z_im[:half] + z_im[half:]], 0)
            y_o = jnp.concatenate([z_re[:half] - z_re[half:], z_im[:half] - z_im[half:]], 0)
            f_e = left_mul(wide[0], y_e)
            f_o = left_mul(wide[1], y_o)
            far[s, k, 0] = f_e
            far[s, k, 1] = f_o
            pow_e = pow_e + (f_e[:half] * f_e[:half] + f_e[half:] * f_e[half:])
            pow_o = pow_o + (f_o[:half] * f_o[:half] + f_o[half:] * f_o[half:])
        pw[s, :half] = pow_e
        pw[s, half:] = pow_o
        swap_power(s).start()

    def back(s, k):
        fac = meas[s]
        fac_e = jnp.concatenate([fac[:half], fac[:half]], 0)
        fac_o = jnp.concatenate([fac[half:], fac[half:]], 0)
        q_e = left_mul(wide[2], far[s, k, 0] * fac_e)
        q_o = left_mul(wide[3], far[s, k, 1] * fac_o)
        up, low = q_e + q_o, q_e - q_o
        w_re = jnp.concatenate([up[:half], low[:half]], 0)
        w_im = jnp.concatenate([up[half:], low[half:]], 0)
        s_e = right_mul(jnp.concatenate([w_re[:, :half], w_im[:, :half]], 1), tall[2])
        s_o = right_mul(jnp.concatenate([w_re[:, half:], w_im[:, half:]], 1), tall[3])
        fst, snd = s_e + s_o, s_e - s_o
        b_re = jnp.concatenate([fst[:, :half], snd[:, :half]], 1)
        b_im = jnp.concatenate([fst[:, half:], snd[:, half:]], 1)
        a_re, a_im = patch[s, 0], patch[s, 1]
        acc[0, k] += a_re * b_re + a_im * b_im
        acc[1, k] += a_re * b_im - a_im * b_re
        p_re, p_im = probe[0, k], probe[1, k]
        return p_re * b_re + p_im * b_im, p_re * b_im - p_im * b_re

    @pl.loop(0, cap)
    def _(s):
        swap_power(s).wait_recv()
        live = jnp.where(s < cnt_ref[0], 1.0, 0.0).astype(F32)
        meas[s] = live * (1.0 - meas[s] * lax.rsqrt(jnp.maximum(pw[s] + pwr[s], 0.25)))
        g_re, g_im = back(s, 0)
        gp[s, 0] = g_re
        gp[s, 1] = g_im

    bits = [b for b in reversed(range(nx.bit_length() - 1))]
    steps = len(bits)
    per = 2 * steps + 2 * (ny - 1)
    los, size = [], 2 * side
    lo = 0
    for b in bits:
        size //= 2
        hb = lax.rem(u // (1 << b), 2)
        los.append((lo + (1 - hb) * size, lo + hb * size, size, b))
        lo = lo + hb * size
    cut = max(1, 8 * ny // size)
    prow, pcol = size * cut // ny, side // cut

    def view(ref, k, at, n):
        return ref.at[at // side, k, pl.ds(pl.multiple_of(lax.rem(at, side), 8), n)]

    def flip(b):
        bit = 1 << b
        return (u + bit - 2 * bit * lax.rem(u // bit, 2), v, m)

    def zplace(ref, k, at):
        r = lax.rem(lo, side) + (at // cut) * prow
        return ref.at[lo // side, k, pl.ds(pl.multiple_of(r, 8), prow),
                      pl.ds(pl.multiple_of(lax.rem(at, cut) * pcol, 128), pcol)]

    def rs(k, n):
        away, mine, sz, b = los[n]
        return remote(view(acc, k, away, sz), rg.at[k, pl.ds(2 * side - 2 * sz, sz)],
                      as_.at[k * per + n], ar.at[k * per + n], flip(b))

    def rs_add(k, n):
        away, mine, sz, b = los[n]
        rs(k, n).wait_recv()
        to = view(acc, k, mine, sz)
        to[...] += rg[k, 2 * side - 2 * sz:2 * side - sz]

    def ag(k, n):
        away, mine, sz, b = los[n]
        at = view(pout, k, mine, sz)
        return remote(at, at, as_.at[k * per + steps + n], ar.at[k * per + steps + n], flip(b))

    def z_rs(k, d):
        to = lax.rem(v + d, ny)
        i = k * per + 2 * steps + d - 1
        return remote(zplace(acc, k, to), rz.at[k, d - 1], as_.at[i], ar.at[i], (u, to, m))

    def z_ag(k, d):
        to = lax.rem(v + d, ny)
        i = k * per + 2 * steps + ny - 1 + d - 1
        at = zplace(pout, k, v)
        return remote(at, at, as_.at[i], ar.at[i], (u, to, m))

    def z_start(k):
        for d in range(1, ny):
            z_rs(k, d).start()

    def z_sum(k):
        total = zplace(acc, k, v)[...]
        for d in range(1, ny):
            z_rs(k, d).wait_recv()
            total = total + rz[k, d - 1]
        zplace(pout, k, v)[...] = total
        for d in range(1, ny):
            z_ag(k, d).start()

    def z_done(k):
        for d in range(1, ny):
            z_ag(k, d).wait_recv()

    rs(0, 0).start()

    def swap_grad(s):
        return remote(gp.at[s, o], gr.at[s], gs.at[s], grs.at[s], other)

    def last_mode(s):
        g_re, g_im = back(s, pm - 1)
        gp[s, 0] += g_re
        gp[s, 1] += g_im
        swap_grad(s).start()

    def put(s):
        swap_grad(s).wait_recv()
        drop, top, shift, base = corner_of(s)
        place = lax.broadcasted_iota(jnp.int32, (side, wide_cols), 0)
        target = lax.broadcasted_iota(jnp.int32, (side, wide_cols), 1)
        move = jnp.where(target == place + shift, 1.0, 0.0).astype(BF16)
        value = jnp.concatenate(split(gp[s, m] + gr[s]), 1)
        x = jnp.dot(value, jnp.concatenate([move, move], 0), preferred_element_type=F32)
        x = jnp.concatenate([x, jnp.zeros((8, wide_cols), F32)], 0)
        for b in (4, 2, 1):
            x = jnp.where(bit_of(drop, b), pltpu.roll(x, b, 0), x)
        zbuf[rows - 8:rows + side, side:side + wide_cols] = x

        @pl.loop(0, (rows + side) // 64)
        def _(i):
            at = pl.multiple_of(i * 64, 8)
            grad[pl.ds(at, 64), :] += zbuf[pl.ds((rows // 8 - 1 + i * 8 - top) * 8, 64),
                                           pl.ds((side // 128 - base) * 128, cols + side)]

    last_mode(0)

    @pl.loop(1, cap // 2)
    def _(s):
        last_mode(s)
        put(s - 1)
    rs_add(0, 0)
    rs(0, 1).start()

    @pl.loop(cap // 2, cap)
    def _(s):
        last_mode(s)
        put(s - 1)
    rs(1, 0).start()
    put(cap - 1)

    c_c = remote(grad.at[rows:rows + side, cols:cols + side], r_c, es.at[0], er.at[0], down_dev)
    c_b = remote(grad.at[rows:rows + side, 0:cols], r_b, es.at[1], er.at[1], down_dev)
    c_r = remote(grad.at[0:rows, cols:cols + side], r_r, es.at[2], er.at[2], right_dev)
    c_d = remote(r_c, r_d, es.at[3], er.at[3], right_dev)

    @pl.when(below)
    def _():
        c_c.start()
        c_b.start()

    @pl.when(right)
    def _():
        c_r.start()
    rs_add(0, 1)
    z_start(0)
    rs_add(1, 0)
    rs(1, 1).start()

    @pl.when(u > 0)
    def _():
        c_c.wait_recv()

        @pl.when(right)
        def _():
            c_d.start()
    z_sum(0)
    rs_add(1, 1)
    z_start(1)
    z_done(0)
    ag(0, 1).start()
    z_sum(1)
    ag(0, 1).wait_recv()
    ag(0, 0).start()
    z_done(1)
    ag(1, 1).start()
    ag(1, 1).wait_recv()
    ag(1, 0).start()

    fin[...] = grad[0:rows, 0:cols]

    @pl.when(v > 0)
    def _():
        c_r.wait_recv()
        fin[:, 0:side] += r_r[...]

    @pl.when(u > 0)
    def _():
        c_b.wait_recv()
        fin[0:side, :] += r_b[...]

    @pl.when((u > 0) & (v > 0))
    def _():
        c_d.wait_recv()
        fin[0:side, 0:side] += r_d[...]
    hrow = rows // 2
    swap = remote(fin.at[pl.ds(pl.multiple_of(o * hrow, 8), hrow)], out.at[m], es.at[4], er.at[4], other)
    swap.start()
    out[m] = fin[pl.ds(pl.multiple_of(m * hrow, 8), hrow), :]
    swap.wait_recv()
    for k in range(pm):
        ag(k, 0).wait_recv()

    for n, (src, place, goes, comes, target) in enumerate(hops):
        @pl.when(goes)
        def _(n=n):
            outs[n].wait_send()

        @pl.when(comes)
        def _(n=n):
            fwds[n].wait_send()

    @pl.loop(0, cap)
    def _(s):
        swap_power(s).wait_send()
        swap_grad(s).wait_send()
    for k in range(pm):
        for n in range(steps):
            rs(k, n).wait_send()
            ag(k, n).wait_send()
        for d in range(1, ny):
            z_rs(k, d).wait_send()
            z_ag(k, d).wait_send()
    swap.wait_send()

    @pl.when(below)
    def _():
        c_c.wait_send()
        c_b.wait_send()

    @pl.when(right)
    def _():
        c_r.wait_send()

    @pl.when((u > 0) & right)
    def _():
        c_d.wait_send()


def local(nx, ny, object_field, probe, offsets, counts, amplitude):
    side = probe.shape[2]
    pm = probe.shape[1]
    rows, cols = object_field.shape[1:]
    cap = offsets.shape[2]
    dma = pltpu.SemaphoreType.DMA
    tall, wide, picks = tables(side)
    steps = nx.bit_length() - 1
    per = 2 * steps + 2 * (ny - 1)
    size = 2 * side // nx
    cut = max(1, 8 * ny // size)

    def vm(*shape):
        return pltpu.VMEM(shape, F32)
    return pl.pallas_call(
        functools.partial(fused_kernel, nx, ny),
        name="fused",
        out_shape=(jax.ShapeDtypeStruct((2, rows // 2, cols), F32), jax.ShapeDtypeStruct((2, pm, side, side), F32)),
        in_specs=[SM, SM, ANY, ANY, ANY, ANY, ANY, ANY],
        out_specs=(VM, VM),
        scratch_shapes=[
            vm(2, rows + side, cols + side), vm(2, pm, side, side), vm(cap, side, side),
            pltpu.VMEM(tall.shape, BF16), pltpu.VMEM(wide.shape, BF16), pltpu.VMEM(picks.shape, BF16),
            vm(cap, 2, side, side), vm(cap, pm, 2, side, side), vm(cap, side, side), vm(cap, side, side),
            vm(cap, 2, side, side), vm(cap, side, side), vm(2 * (rows - 8) + side + 8, cols + 2 * side),
            vm(rows + side, cols + side),
            vm(2, pm, side, side), vm(pm, 2 * side, side), vm(pm, ny - 1, size * cut // ny, side // cut),
            vm(rows, side), vm(side, cols), vm(side, side), vm(side, side), vm(rows, cols),
            dma((6,)), dma((8,)), dma((8,)), dma((cap,)), dma((cap,)), dma((cap,)), dma((cap,)), dma((5,)), dma((5,)),
            dma((pm * per,)), dma((pm * per,)),
        ],
        compiler_params=pltpu.CompilerParams(collective_id=0, has_side_effects=True, vmem_limit_bytes=56 << 20),
    )(offsets[0, 0].T, counts[0], object_field, probe, amplitude,
      jnp.asarray(tall), jnp.asarray(wide), jnp.asarray(picks))


def solution(mesh):
    return jax.shard_map(
        functools.partial(local, mesh.shape["gx"], mesh.shape["gy"]),
        mesh=mesh,
        in_specs=(
            P(None, "gx", "gy"),
            P(None, "ma", None, None),
            P("gx", "gy", None, None),
            P("gx", "gy"),
            P("gx", "gy", None, None, None),
        ),
        out_specs=(P(None, ("gx", "ma"), "gy"), P(None, "ma", None, None)),
        check_vma=False,
    )
```

```python
import functools

import jax
import jax.numpy as jnp
import ml_dtypes
import numpy as np
from jax import lax
from jax.experimental import pallas as pl
from jax.experimental.pallas import tpu as pltpu
from jax.sharding import PartitionSpec as P

F32 = jnp.float32
BF16 = jnp.bfloat16
MESH = pl.DeviceIdType.MESH
ANY = pl.BlockSpec(memory_space=pl.ANY)
SM = pl.BlockSpec(memory_space=pltpu.SMEM)
VM = pl.BlockSpec(memory_space=pltpu.VMEM)


def tables(side):
    half = side // 2
    line = np.arange(half)
    found = []
    for odd in (0, 1):
        product = (2 * line[:, None] + odd) * line[None, :] % side
        value = np.exp(-2j * np.pi * product / side) / np.sqrt(side)
        block = np.block([[value.real, -value.imag], [value.imag, value.real]])
        found.append(block)

    def parts(block):
        high = block.astype(np.float32).astype(ml_dtypes.bfloat16)
        low = (block - high.astype(np.float64)).astype(np.float32).astype(ml_dtypes.bfloat16)
        return high, high, low

    tall = [np.concatenate(parts(b), 0) for b in (found[0].T, found[1].T, found[0], found[1])]
    wide = [np.concatenate(parts(b), 1) for b in (found[0], found[1], found[0].T, found[1].T)]
    order = np.concatenate([np.arange(0, side, 2), np.arange(1, side, 2)])
    pick = np.zeros((side, side), np.float32)
    pick[order, np.arange(side)] = 1.0
    picks = np.stack([pick, pick.T]).astype(ml_dtypes.bfloat16)
    return np.stack(tall), np.stack(wide), picks


def split(x):
    high = x.astype(BF16)
    return high, (x - high.astype(F32)).astype(BF16)


def right_mul(x, table):
    high, low = split(x)
    return jnp.dot(jnp.concatenate([high, low, high], 1), table, preferred_element_type=F32)


def left_mul(table, x):
    high, low = split(x)
    return jnp.dot(table, jnp.concatenate([high, low, high], 0), preferred_element_type=F32)


def remote(src, dst, send, recv, where):
    return pltpu.make_async_remote_copy(src_ref=src, dst_ref=dst, send_sem=send, recv_sem=recv,
                                        device_id=where, device_id_type=MESH)


def fused_kernel(nx, ny, chunks, off_ref, cnt_ref, obj, probe_hbm, amp_hbm, tall_hbm, wide_hbm, pick_hbm,
                 out, pout,
                 ext, probe, meas, tall, wide, pick, patch, far, pw, pwr, gp, gr, zbuf, grad,
                 acc, rg, rz, r_r, r_b, r_c, fin, lsem, hs, hr, ps, pr, gs, grs, es, er, as_, ar):
    u, v, m = lax.axis_index("gx"), lax.axis_index("gy"), lax.axis_index("ma")
    o = 1 - m
    side = probe.shape[2]
    half = side // 2
    pm = probe.shape[1]
    cap = meas.shape[0]
    rows, cols = obj.shape[1], obj.shape[2]
    other = (u, v, o)
    right, below = v < ny - 1, u < nx - 1
    left_dev, right_dev = (u, v - 1, m), (u, v + 1, m)
    up_dev, down_dev = (u - 1, v, m), (u + 1, v, m)

    local = [
        pltpu.make_async_copy(amp_hbm.at[0, 0], meas, lsem.at[0]),
        pltpu.make_async_copy(pick_hbm, pick, lsem.at[1]),
        pltpu.make_async_copy(obj, ext.at[:, 0:rows, 0:cols], lsem.at[2]),
        pltpu.make_async_copy(probe_hbm, probe, lsem.at[3]),
        pltpu.make_async_copy(tall_hbm, tall, lsem.at[4]),
        pltpu.make_async_copy(wide_hbm, wide, lsem.at[5]),
    ]
    for c in local:
        c.start()

    barrier = pltpu.get_barrier_semaphore()

    def greet(where):
        pl.semaphore_signal(barrier, inc=1, device_id=where, device_id_type=MESH)
    greet(other)
    for d in range(1, nx):
        greet((lax.rem(u + d, nx), v, m))
    for d in range(1, ny):
        greet((u, lax.rem(v + d, ny), m))

    @pl.when(jnp.logical_not(right))
    def _():
        ext[:, 0:rows, cols:cols + side] = jnp.zeros((2, rows, side), F32)

    @pl.when(jnp.logical_not(below))
    def _():
        ext[:, rows:rows + side, 0:cols] = jnp.zeros((2, side, cols), F32)

    @pl.when(jnp.logical_not(below & right))
    def _():
        ext[:, rows:rows + side, cols:cols + side] = jnp.zeros((2, side, side), F32)
    pl.semaphore_wait(barrier, nx + ny - 1)

    def piece(ref, r0, rn, c0, cn):
        return ref.at[m, r0:r0 + rn, c0:c0 + cn]

    h = rows - side
    first, rest = (0, side, cols, side), (side, h, cols, side)
    under, corner = (rows, side, 0, cols), (rows, side, cols, side)
    hops = [
        (piece(obj, 0, side, 0, side), first, v > 0, right, left_dev),
        (piece(obj, 0, side, 0, cols), under, u > 0, below, up_dev),
        (piece(obj, side, h, 0, side), rest, v > 0, right, left_dev),
        (piece(ext, *first), corner, (u > 0) & right, below & right, up_dev),
    ]
    outs, fwds = [], []
    for n, (src, place, goes, comes, target) in enumerate(hops):
        outs.append(remote(src, piece(ext, *place), hs.at[n], hr.at[n], target))
        fwds.append(remote(piece(ext, *place), piece(ext, *place), hs.at[4 + n], hr.at[4 + n], other))
    for n in range(3):
        @pl.when(hops[n][2])
        def _(n=n):
            outs[n].start()

    @pl.loop(0, zbuf.shape[0] // 8)
    def _(i):
        zbuf[pl.ds(pl.multiple_of(i * 8, 8), 8), :] = jnp.zeros((8, zbuf.shape[1]), F32)
    grad[...] = jnp.zeros_like(grad)
    acc[...] = jnp.zeros_like(acc)
    local[0].wait()
    local[1].wait()

    @pl.loop(0, cap)
    def _(s):
        measured = jnp.zeros((side, side), F32)
        for term in split(meas[s]):
            moved = jnp.dot(term, pick[0], preferred_element_type=F32).astype(BF16)
            measured = measured + jnp.dot(pick[1], moved, preferred_element_type=F32)
        meas[s] = measured

    for n, (src, place, goes, comes, target) in enumerate(hops):
        @pl.when(comes)
        def _(n=n):
            outs[n].wait_recv()
            if n == 0:
                @pl.when(u > 0)
                def _():
                    outs[3].start()
            fwds[n].start()
    for c in local[2:]:
        c.wait()
    for n, (src, place, goes, comes, target) in enumerate(hops):
        @pl.when(comes)
        def _(n=n):
            fwds[n].wait_recv()

    tall_rows, wide_cols = side + 8, side + 128

    def corner_of(s):
        row, col = off_ref[0, s], off_ref[1, s]
        return lax.rem(row, 8), lax.div(row, 8), lax.rem(col, 128), lax.div(col, 128)

    def swap_power(s):
        return remote(pw.at[s], pwr.at[s], ps.at[s], pr.at[s], other)

    @pl.loop(0, cap)
    def _(s):
        drop, top, shift, base = corner_of(s)

        def take(part):
            x = ext[part, pl.ds(top * 8, tall_rows), pl.ds(base * 128, wide_cols)]
            x = pltpu.roll(x, lax.rem(wide_cols - shift, wide_cols), 1)[:, :side]
            return pltpu.roll(x, lax.rem(tall_rows - drop, tall_rows), 0)[:side]

        a_re, a_im = take(0), take(1)
        patch[s, 0] = a_re
        patch[s, 1] = a_im
        pow_e = pow_o = jnp.zeros((half, side), F32)
        for k in range(pm):
            p_re, p_im = probe[0, k], probe[1, k]
            e_re = p_re * a_re - p_im * a_im
            e_im = p_re * a_im + p_im * a_re
            x_e = jnp.concatenate([e_re[:, :half] + e_re[:, half:], e_im[:, :half] + e_im[:, half:]], 1)
            x_o = jnp.concatenate([e_re[:, :half] - e_re[:, half:], e_im[:, :half] - e_im[:, half:]], 1)
            z_e = right_mul(x_e, tall[0])
            z_o = right_mul(x_o, tall[1])
            z_re = jnp.concatenate([z_e[:, :half], z_o[:, :half]], 1)
            z_im = jnp.concatenate([z_e[:, half:], z_o[:, half:]], 1)
            y_e = jnp.concatenate([z_re[:half] + z_re[half:], z_im[:half] + z_im[half:]], 0)
            y_o = jnp.concatenate([z_re[:half] - z_re[half:], z_im[:half] - z_im[half:]], 0)
            f_e = left_mul(wide[0], y_e)
            f_o = left_mul(wide[1], y_o)
            far[s, k, 0] = f_e
            far[s, k, 1] = f_o
            pow_e = pow_e + (f_e[:half] * f_e[:half] + f_e[half:] * f_e[half:])
            pow_o = pow_o + (f_o[:half] * f_o[:half] + f_o[half:] * f_o[half:])
        pw[s, :half] = pow_e
        pw[s, half:] = pow_o
        swap_power(s).start()

    def back(s, k):
        fac = meas[s]
        fac_e = jnp.concatenate([fac[:half], fac[:half]], 0)
        fac_o = jnp.concatenate([fac[half:], fac[half:]], 0)
        q_e = left_mul(wide[2], far[s, k, 0] * fac_e)
        q_o = left_mul(wide[3], far[s, k, 1] * fac_o)
        up, low = q_e + q_o, q_e - q_o
        w_re = jnp.concatenate([up[:half], low[:half]], 0)
        w_im = jnp.concatenate([up[half:], low[half:]], 0)
        s_e = right_mul(jnp.concatenate([w_re[:, :half], w_im[:, :half]], 1), tall[2])
        s_o = right_mul(jnp.concatenate([w_re[:, half:], w_im[:, half:]], 1), tall[3])
        fst, snd = s_e + s_o, s_e - s_o
        b_re = jnp.concatenate([fst[:, :half], snd[:, :half]], 1)
        b_im = jnp.concatenate([fst[:, half:], snd[:, half:]], 1)
        a_re, a_im = patch[s, 0], patch[s, 1]
        acc[0, k] += (a_re * b_re + a_im * b_im).reshape(2, half, side)
        acc[1, k] += (a_re * b_im - a_im * b_re).reshape(2, half, side)
        p_re, p_im = probe[0, k], probe[1, k]
        return p_re * b_re + p_im * b_im, p_re * b_im - p_im * b_re

    @pl.loop(0, cap)
    def _(s):
        swap_power(s).wait_recv()
        live = jnp.where(s < cnt_ref[0], 1.0, 0.0).astype(F32)
        meas[s] = live * (1.0 - meas[s] * lax.rsqrt(jnp.maximum(pw[s] + pwr[s], 0.25)))
        g_re, g_im = back(s, 0)
        gp[s, 0] = g_re
        gp[s, 1] = g_im

    slab = half // chunks
    hy, hx = u // 2, lax.rem(u, 2)
    by_y, by_x = (lax.rem(u + 2, 4), v, m), (u + 1 - 2 * hx, v, m)
    per = 4 + 2 * (ny - 1)
    cut = max(1, 8 * ny // slab)
    prow, pcol = slab * cut // ny, side // cut

    def across(q):
        return q // chunks, pl.ds(q % chunks * slab, slab)

    def x_leads(q):
        return False

    def rs(q, n):
        k, c = across(q)
        if x_leads(q):
            src, to = (acc.at[:, k, 1 - hx, c], by_x) if n == 0 else (acc.at[1 - hy, k, hx, c], by_y)
        else:
            src, to = (acc.at[1 - hy, k, :, c], by_y) if n == 0 else (acc.at[hy, k, 1 - hx, c], by_x)
        return remote(src, rg.at[k, 0:2, c] if n == 0 else rg.at[k, 2, c],
                      as_.at[q * per + n], ar.at[q * per + n], to)

    def first(q):
        k, c = across(q)
        rs(q, 0).wait_recv()
        if x_leads(q):
            acc[:, k, hx, c] += rg[k, 0:2, c]
        else:
            acc[hy, k, :, c] += rg[k, 0:2, c]
        rs(q, 1).start()

    def zplace(ref, q, at):
        k = q // chunks
        r = q % chunks * slab + (at // cut) * prow
        c = lax.rem(at, cut) * pcol
        return ref.at[hy, k, hx, pl.ds(pl.multiple_of(r, 8), prow), pl.ds(pl.multiple_of(c, 128), pcol)]

    def z_rs(q, d):
        to = lax.rem(v + d, ny)
        i = q * per + 4 + d - 1
        return remote(zplace(acc, q, to), rz.at[q, d - 1], as_.at[i], ar.at[i], (u, to, m))

    def z_ag(q, d):
        to = lax.rem(v + d, ny)
        i = q * per + 4 + ny - 1 + d - 1
        at = zplace(pout, q, v)
        return remote(at, at, as_.at[i], ar.at[i], (u, to, m))

    def second(q):
        k, c = across(q)
        rs(q, 1).wait_recv()
        acc[hy, k, hx, c] += rg[k, 2, c]
        for d in range(1, ny):
            z_rs(q, d).start()

    def z_sum(q):
        total = zplace(acc, q, v)[...]
        for d in range(1, ny):
            z_rs(q, d).wait_recv()
            total = total + rz[q, d - 1]
        zplace(pout, q, v)[...] = total
        for d in range(1, ny):
            z_ag(q, d).start()

    def ag(q, n):
        k, c = across(q)
        x_first = q % chunks == 0
        if n == 0:
            at, to = pout.at[hy, k, hx, c], by_x if x_first else by_y
        elif x_first:
            at, to = pout.at[hy, k, :, c], by_y
        else:
            at, to = pout.at[:, k, hx, c], by_x
        return remote(at, at, as_.at[q * per + 2 + n], ar.at[q * per + 2 + n], to)

    def gather(q):
        for d in range(1, ny):
            z_ag(q, d).wait_recv()
        ag(q, 0).start()

    def spread(q):
        ag(q, 0).wait_recv()
        ag(q, 1).start()

    early, late = range(chunks), range(chunks, 2 * chunks)
    for q in early:
        rs(q, 0).start()

    def swap_grad(s):
        return remote(gp.at[s, o], gr.at[s], gs.at[s], grs.at[s], other)

    def last_mode(s):
        g_re, g_im = back(s, pm - 1)
        gp[s, 0] += g_re
        gp[s, 1] += g_im
        swap_grad(s).start()

    def put(s):
        swap_grad(s).wait_recv()
        drop, top, shift, base = corner_of(s)
        value = gp[s, m] + gr[s]
        x = pltpu.roll(jnp.concatenate([value, jnp.zeros((8, side), F32)], 0), drop, 0)
        x = jnp.concatenate([x, jnp.zeros((tall_rows, 128), F32)], 1)
        zbuf[rows - 8:rows + side, side:side + wide_cols] = pltpu.roll(x, shift, 1)

        @pl.loop(0, (rows + side) // 64)
        def _(i):
            at = pl.multiple_of(i * 64, 8)
            grad[pl.ds(at, 64), :] += zbuf[pl.ds((rows // 8 - 1 + i * 8 - top) * 8, 64),
                                           pl.ds((side // 128 - base) * 128, cols + side)]

    last_mode(0)

    @pl.loop(1, cap)
    def _(s):
        last_mode(s)
    for q in late:
        rs(q, 0).start()

    @pl.loop(0, cap)
    def _(s):
        put(s)

    def edge(i, src, dst, to):
        return remote(src, dst, es.at[i], er.at[i], to)
    quart = side // 4
    c_c = [edge(i, grad.at[rows + i * half:rows + (i + 1) * half, cols:cols + side],
                r_c.at[i * half:(i + 1) * half], down_dev) for i in range(2)]
    c_t = [edge(2 + i, grad.at[i * half:(i + 1) * half, cols:cols + side],
                r_r.at[i * half:(i + 1) * half], right_dev) for i in range(2)]
    span = (rows - side) // 2
    c_l = [edge(4 + i, grad.at[side + i * span:side + (i + 1) * span, cols:cols + side],
                r_r.at[side + i * span:side + (i + 1) * span], right_dev) for i in range(2)]
    c_b = [edge(6 + i, grad.at[rows + i * quart:rows + (i + 1) * quart, 0:cols],
                r_b.at[i * quart:(i + 1) * quart], down_dev) for i in range(4)]

    def send(copies, when):
        @pl.when(when)
        def _():
            for c in copies:
                c.start()

    def merge(i):
        @pl.when(right & (u > 0))
        def _():
            c_c[i].wait_recv()
            grad[i * half:(i + 1) * half, cols:cols + side] += r_c[i * half:(i + 1) * half]
        send([c_t[i]], right)

    for q in early:
        first(q)
    send(c_c[:1], below & right)
    send(c_l[:1], right)
    send(c_c[1:], below & right)
    for q in early:
        second(q)
    send(c_l[1:], right)
    for q in late:
        first(q)
    send(c_b[:1], below)
    for q in early:
        z_sum(q)
    send(c_b[1:2], below)
    merge(0)
    for q in late:
        second(q)
    merge(1)
    send(c_b[2:3], below)
    for q in early:
        gather(q)
    send(c_b[3:], below)
    for q in late:
        z_sum(q)
    for q in early:
        spread(q)
    for q in late:
        gather(q)

    fin[...] = grad[0:rows, 0:cols]

    @pl.when(v > 0)
    def _():
        for c in c_l + c_t:
            c.wait_recv()
        fin[:, 0:side] += r_r[...]

    @pl.when(u > 0)
    def _():
        for c in c_b:
            c.wait_recv()
        fin[0:side, :] += r_b[...]

    hrow = rows // 2
    swap = remote(fin.at[pl.ds(pl.multiple_of(o * hrow, 8), hrow)], out.at[m], es.at[10], er.at[10], other)
    swap.start()
    out[m] = fin[pl.ds(pl.multiple_of(m * hrow, 8), hrow), :]
    for q in late:
        spread(q)
    swap.wait_recv()
    for q in (*early, *late):
        ag(q, 1).wait_recv()

    for n, (src, place, goes, comes, target) in enumerate(hops):
        @pl.when(goes)
        def _(n=n):
            outs[n].wait_send()

        @pl.when(comes)
        def _(n=n):
            fwds[n].wait_send()

    @pl.loop(0, cap)
    def _(s):
        swap_power(s).wait_send()
        swap_grad(s).wait_send()
    for q in (*early, *late):
        for c in (rs(q, 0), rs(q, 1), ag(q, 0), ag(q, 1)):
            c.wait_send()
        for d in range(1, ny):
            z_rs(q, d).wait_send()
            z_ag(q, d).wait_send()
    swap.wait_send()

    @pl.when(below)
    def _():
        for c in c_b:
            c.wait_send()

    @pl.when(right)
    def _():
        for c in c_l + c_t:
            c.wait_send()

    @pl.when(below & right)
    def _():
        for c in c_c:
            c.wait_send()


def local(nx, ny, object_field, probe, offsets, counts, amplitude):
    side = probe.shape[2]
    pm = probe.shape[1]
    rows, cols = object_field.shape[1:]
    cap = offsets.shape[2]
    dma = pltpu.SemaphoreType.DMA
    tall, wide, picks = tables(side)
    half = side // 2
    chunks = 2 if ny <= half // 16 else 1
    per = 4 + 2 * (ny - 1)
    slab = half // chunks
    cut = max(1, 8 * ny // slab)
    parts = pm * chunks
    assert nx == 4 and pm == 2

    def vm(*shape):
        return pltpu.VMEM(shape, F32)
    grad, pg = pl.pallas_call(
        functools.partial(fused_kernel, nx, ny, chunks),
        name="fused",
        out_shape=(jax.ShapeDtypeStruct((2, rows // 2, cols), F32), jax.ShapeDtypeStruct((2, pm, 2, half, side), F32)),
        in_specs=[SM, SM, ANY, ANY, ANY, ANY, ANY, ANY],
        out_specs=(VM, VM),
        scratch_shapes=[
            vm(2, rows + side, cols + side), vm(2, pm, side, side), vm(cap, side, side),
            pltpu.VMEM(tall.shape, BF16), pltpu.VMEM(wide.shape, BF16), pltpu.VMEM(picks.shape, BF16),
            vm(cap, 2, side, side), vm(cap, pm, 2, side, side), vm(cap, side, side), vm(cap, side, side),
            vm(cap, 2, side, side), vm(cap, side, side), vm(2 * (rows - 8) + side + 8, cols + 2 * side),
            vm(rows + side, cols + side),
            vm(2, pm, 2, half, side), vm(pm, 3, half, side), vm(parts, ny - 1, slab * cut // ny, side // cut),
            vm(rows, side), vm(side, cols), vm(side, side), vm(rows, cols),
            dma((6,)), dma((8,)), dma((8,)), dma((cap,)), dma((cap,)), dma((cap,)), dma((cap,)), dma((11,)), dma((11,)),
            dma((parts * per,)), dma((parts * per,)),
        ],
        compiler_params=pltpu.CompilerParams(collective_id=0, has_side_effects=True, vmem_limit_bytes=56 << 20),
    )(offsets[0, 0].T, counts[0], object_field, probe, amplitude,
      jnp.asarray(tall), jnp.asarray(wide), jnp.asarray(picks))
    return grad, pg.reshape(2, pm, side, side)


def solution(mesh):
    return jax.shard_map(
        functools.partial(local, mesh.shape["gx"], mesh.shape["gy"]),
        mesh=mesh,
        in_specs=(
            P(None, "gx", "gy"),
            P(None, "ma", None, None),
            P("gx", "gy", None, None),
            P("gx", "gy"),
            P("gx", "gy", None, None, None),
        ),
        out_specs=(P(None, ("gx", "ma"), "gy"), P(None, "ma", None, None)),
        check_vma=False,
    )
```

```python
import functools

import jax
import jax.numpy as jnp
import ml_dtypes
import numpy as np
from jax import lax
from jax.experimental import pallas as pl
from jax.experimental.pallas import tpu as pltpu
from jax.sharding import PartitionSpec as P

F32 = jnp.float32
BF16 = jnp.bfloat16
MESH = pl.DeviceIdType.MESH
ANY = pl.BlockSpec(memory_space=pl.ANY)
SM = pl.BlockSpec(memory_space=pltpu.SMEM)
VM = pl.BlockSpec(memory_space=pltpu.VMEM)


def tables(side):
    half = side // 2
    line = np.arange(half)
    found = []
    for odd in (0, 1):
        product = (2 * line[:, None] + odd) * line[None, :] % side
        value = np.exp(-2j * np.pi * product / side) / np.sqrt(side)
        block = np.block([[value.real, -value.imag], [value.imag, value.real]])
        found.append(block)

    def parts(block):
        high = block.astype(np.float32).astype(ml_dtypes.bfloat16)
        low = (block - high.astype(np.float64)).astype(np.float32).astype(ml_dtypes.bfloat16)
        return high, high, low

    tall = [np.concatenate(parts(b), 0) for b in (found[0].T, found[1].T, found[0], found[1])]
    wide = [np.concatenate(parts(b), 1) for b in (found[0], found[1], found[0].T, found[1].T)]
    order = np.concatenate([np.arange(0, side, 2), np.arange(1, side, 2)])
    pick = np.zeros((side, side), np.float32)
    pick[order, np.arange(side)] = 1.0
    picks = np.stack([pick, pick.T]).astype(ml_dtypes.bfloat16)
    return np.stack(tall), np.stack(wide), picks


def split(x):
    high = x.astype(BF16)
    return high, (x - high.astype(F32)).astype(BF16)


def right_mul(x, table):
    high, low = split(x)
    return jnp.dot(jnp.concatenate([high, low, high], 1), table, preferred_element_type=F32)


def left_mul(table, x):
    high, low = split(x)
    return jnp.dot(table, jnp.concatenate([high, low, high], 0), preferred_element_type=F32)


def remote(src, dst, send, recv, where):
    return pltpu.make_async_remote_copy(src_ref=src, dst_ref=dst, send_sem=send, recv_sem=recv,
                                        device_id=where, device_id_type=MESH)


def fused_kernel(nx, ny, chunks, off_ref, cnt_ref, obj, probe_hbm, amp_hbm, tall_hbm, wide_hbm, pick_hbm,
                 out, pout,
                 ext, probe, meas, tall, wide, pick, patch, far, pw, pwr, gp, gr, zbuf, grad,
                 acc, rg, rz, r_r, r_b, r_c, fin, lsem, hs, hr, ps, pr, gs, grs, es, er, as_, ar):
    u, v, m = lax.axis_index("gx"), lax.axis_index("gy"), lax.axis_index("ma")
    o = 1 - m
    side = probe.shape[2]
    half = side // 2
    pm = probe.shape[1]
    cap = meas.shape[0]
    rows, cols = obj.shape[1], obj.shape[2]
    other = (u, v, o)
    right, below = v < ny - 1, u < nx - 1
    left_dev, right_dev = (u, v - 1, m), (u, v + 1, m)
    up_dev, down_dev = (u - 1, v, m), (u + 1, v, m)

    local = [
        pltpu.make_async_copy(amp_hbm.at[0, 0], meas, lsem.at[0]),
        pltpu.make_async_copy(pick_hbm, pick, lsem.at[1]),
        pltpu.make_async_copy(obj, ext.at[:, 0:rows, 0:cols], lsem.at[2]),
        pltpu.make_async_copy(probe_hbm, probe, lsem.at[3]),
        pltpu.make_async_copy(tall_hbm, tall, lsem.at[4]),
        pltpu.make_async_copy(wide_hbm, wide, lsem.at[5]),
    ]
    for c in local:
        c.start()

    barrier = pltpu.get_barrier_semaphore()

    def greet(where):
        pl.semaphore_signal(barrier, inc=1, device_id=where, device_id_type=MESH)
    greet(other)
    for d in range(1, nx):
        greet((lax.rem(u + d, nx), v, m))
    for d in range(1, ny):
        greet((u, lax.rem(v + d, ny), m))

    @pl.when(jnp.logical_not(right))
    def _():
        ext[:, 0:rows, cols:cols + side] = jnp.zeros((2, rows, side), F32)

    @pl.when(jnp.logical_not(below))
    def _():
        ext[:, rows:rows + side, 0:cols] = jnp.zeros((2, side, cols), F32)

    @pl.when(jnp.logical_not(below & right))
    def _():
        ext[:, rows:rows + side, cols:cols + side] = jnp.zeros((2, side, side), F32)
    pl.semaphore_wait(barrier, nx + ny - 1)

    def piece(ref, r0, rn, c0, cn):
        return ref.at[m, r0:r0 + rn, c0:c0 + cn]

    h = rows - side
    first, rest = (0, side, cols, side), (side, h, cols, side)
    under, corner = (rows, side, 0, cols), (rows, side, cols, side)
    hops = [
        (piece(obj, 0, side, 0, side), first, v > 0, right, left_dev),
        (piece(obj, 0, side, 0, cols), under, u > 0, below, up_dev),
        (piece(obj, side, h, 0, side), rest, v > 0, right, left_dev),
        (piece(ext, *first), corner, (u > 0) & right, below & right, up_dev),
    ]
    outs, fwds = [], []
    for n, (src, place, goes, comes, target) in enumerate(hops):
        outs.append(remote(src, piece(ext, *place), hs.at[n], hr.at[n], target))
        fwds.append(remote(piece(ext, *place), piece(ext, *place), hs.at[4 + n], hr.at[4 + n], other))
    for n in range(3):
        @pl.when(hops[n][2])
        def _(n=n):
            outs[n].start()

    @pl.loop(0, zbuf.shape[0] // 8)
    def _(i):
        zbuf[pl.ds(pl.multiple_of(i * 8, 8), 8), :] = jnp.zeros((8, zbuf.shape[1]), F32)
    grad[...] = jnp.zeros_like(grad)
    acc[...] = jnp.zeros_like(acc)
    local[0].wait()
    local[1].wait()

    @pl.loop(0, cap)
    def _(s):
        measured = jnp.zeros((side, side), F32)
        for term in split(meas[s]):
            moved = jnp.dot(term, pick[0], preferred_element_type=F32).astype(BF16)
            measured = measured + jnp.dot(pick[1], moved, preferred_element_type=F32)
        meas[s] = measured

    for n, (src, place, goes, comes, target) in enumerate(hops):
        @pl.when(comes)
        def _(n=n):
            outs[n].wait_recv()
            if n == 0:
                @pl.when(u > 0)
                def _():
                    outs[3].start()
            fwds[n].start()
    for c in local[2:]:
        c.wait()
    for n, (src, place, goes, comes, target) in enumerate(hops):
        @pl.when(comes)
        def _(n=n):
            fwds[n].wait_recv()

    tall_rows, wide_cols = side + 8, side + 128

    def corner_of(s):
        row, col = off_ref[0, s], off_ref[1, s]
        return lax.rem(row, 8), lax.div(row, 8), lax.rem(col, 128), lax.div(col, 128)

    def swap_power(s):
        return remote(pw.at[s], pwr.at[s], ps.at[s], pr.at[s], other)

    @pl.loop(0, cap)
    def _(s):
        drop, top, shift, base = corner_of(s)

        def take(part):
            x = ext[part, pl.ds(top * 8, tall_rows), pl.ds(base * 128, wide_cols)]
            x = pltpu.roll(x, lax.rem(wide_cols - shift, wide_cols), 1)[:, :side]
            return pltpu.roll(x, lax.rem(tall_rows - drop, tall_rows), 0)[:side]

        a_re, a_im = take(0), take(1)
        patch[s, 0] = a_re
        patch[s, 1] = a_im
        pow_e = pow_o = jnp.zeros((half, side), F32)
        for k in range(pm):
            p_re, p_im = probe[0, k], probe[1, k]
            e_re = p_re * a_re - p_im * a_im
            e_im = p_re * a_im + p_im * a_re
            x_e = jnp.concatenate([e_re[:, :half] + e_re[:, half:], e_im[:, :half] + e_im[:, half:]], 1)
            x_o = jnp.concatenate([e_re[:, :half] - e_re[:, half:], e_im[:, :half] - e_im[:, half:]], 1)
            z_e = right_mul(x_e, tall[0])
            z_o = right_mul(x_o, tall[1])
            z_re = jnp.concatenate([z_e[:, :half], z_o[:, :half]], 1)
            z_im = jnp.concatenate([z_e[:, half:], z_o[:, half:]], 1)
            y_e = jnp.concatenate([z_re[:half] + z_re[half:], z_im[:half] + z_im[half:]], 0)
            y_o = jnp.concatenate([z_re[:half] - z_re[half:], z_im[:half] - z_im[half:]], 0)
            f_e = left_mul(wide[0], y_e)
            f_o = left_mul(wide[1], y_o)
            far[s, k, 0] = f_e
            far[s, k, 1] = f_o
            pow_e = pow_e + (f_e[:half] * f_e[:half] + f_e[half:] * f_e[half:])
            pow_o = pow_o + (f_o[:half] * f_o[:half] + f_o[half:] * f_o[half:])
        pw[s, :half] = pow_e
        pw[s, half:] = pow_o
        swap_power(s).start()

    def back(s, k):
        fac = meas[s]
        fac_e = jnp.concatenate([fac[:half], fac[:half]], 0)
        fac_o = jnp.concatenate([fac[half:], fac[half:]], 0)
        q_e = left_mul(wide[2], far[s, k, 0] * fac_e)
        q_o = left_mul(wide[3], far[s, k, 1] * fac_o)
        up, low = q_e + q_o, q_e - q_o
        w_re = jnp.concatenate([up[:half], low[:half]], 0)
        w_im = jnp.concatenate([up[half:], low[half:]], 0)
        s_e = right_mul(jnp.concatenate([w_re[:, :half], w_im[:, :half]], 1), tall[2])
        s_o = right_mul(jnp.concatenate([w_re[:, half:], w_im[:, half:]], 1), tall[3])
        fst, snd = s_e + s_o, s_e - s_o
        b_re = jnp.concatenate([fst[:, :half], snd[:, :half]], 1)
        b_im = jnp.concatenate([fst[:, half:], snd[:, half:]], 1)
        a_re, a_im = patch[s, 0], patch[s, 1]
        acc[0, k] += (a_re * b_re + a_im * b_im).reshape(2, half, side)
        acc[1, k] += (a_re * b_im - a_im * b_re).reshape(2, half, side)
        p_re, p_im = probe[0, k], probe[1, k]
        return p_re * b_re + p_im * b_im, p_re * b_im - p_im * b_re

    @pl.loop(0, cap)
    def _(s):
        swap_power(s).wait_recv()
        live = jnp.where(s < cnt_ref[0], 1.0, 0.0).astype(F32)
        meas[s] = live * (1.0 - meas[s] * lax.rsqrt(jnp.maximum(pw[s] + pwr[s], 0.25)))
        g_re, g_im = back(s, 0)
        gp[s, 0] = g_re
        gp[s, 1] = g_im

    slab = half // chunks
    hy, hx = u // 2, lax.rem(u, 2)
    by_y, by_x = (lax.rem(u + 2, 4), v, m), (u + 1 - 2 * hx, v, m)
    per = 4 + 2 * (ny - 1)
    cut = max(1, 8 * ny // slab)
    prow, pcol = slab * cut // ny, side // cut

    def across(q):
        return q // chunks, pl.ds(q % chunks * slab, slab)

    def x_leads(q):
        return q % chunks == 1

    def rs(q, n):
        k, c = across(q)
        if x_leads(q):
            src, to = (acc.at[:, k, 1 - hx, c], by_x) if n == 0 else (acc.at[1 - hy, k, hx, c], by_y)
        else:
            src, to = (acc.at[1 - hy, k, :, c], by_y) if n == 0 else (acc.at[hy, k, 1 - hx, c], by_x)
        return remote(src, rg.at[k, 0:2, c] if n == 0 else rg.at[k, 2, c],
                      as_.at[q * per + n], ar.at[q * per + n], to)

    def first(q):
        k, c = across(q)
        rs(q, 0).wait_recv()
        if x_leads(q):
            acc[:, k, hx, c] += rg[k, 0:2, c]
        else:
            acc[hy, k, :, c] += rg[k, 0:2, c]
        rs(q, 1).start()

    def zplace(ref, q, at):
        k = q // chunks
        r = q % chunks * slab + (at // cut) * prow
        c = lax.rem(at, cut) * pcol
        return ref.at[hy, k, hx, pl.ds(pl.multiple_of(r, 8), prow), pl.ds(pl.multiple_of(c, 128), pcol)]

    def z_rs(q, d):
        to = lax.rem(v + d, ny)
        i = q * per + 4 + d - 1
        return remote(zplace(acc, q, to), rz.at[q, d - 1], as_.at[i], ar.at[i], (u, to, m))

    def z_ag(q, d):
        to = lax.rem(v + d, ny)
        i = q * per + 4 + ny - 1 + d - 1
        at = zplace(pout, q, v)
        return remote(at, at, as_.at[i], ar.at[i], (u, to, m))

    def second(q):
        k, c = across(q)
        rs(q, 1).wait_recv()
        acc[hy, k, hx, c] += rg[k, 2, c]
        for d in range(1, ny):
            z_rs(q, d).start()

    def z_sum(q):
        total = zplace(acc, q, v)[...]
        for d in range(1, ny):
            z_rs(q, d).wait_recv()
            total = total + rz[q, d - 1]
        zplace(pout, q, v)[...] = total
        for d in range(1, ny):
            z_ag(q, d).start()

    def ag(q, n):
        k, c = across(q)
        x_first = q % chunks == 0
        if n == 0:
            at, to = pout.at[hy, k, hx, c], by_x if x_first else by_y
        elif x_first:
            at, to = pout.at[hy, k, :, c], by_y
        else:
            at, to = pout.at[:, k, hx, c], by_x
        return remote(at, at, as_.at[q * per + 2 + n], ar.at[q * per + 2 + n], to)

    def gather(q):
        for d in range(1, ny):
            z_ag(q, d).wait_recv()
        ag(q, 0).start()

    def spread(q):
        ag(q, 0).wait_recv()
        ag(q, 1).start()

    early, late = range(chunks), range(chunks, 2 * chunks)
    for q in early:
        rs(q, 0).start()

    def swap_grad(s):
        return remote(gp.at[s, o], gr.at[s], gs.at[s], grs.at[s], other)

    def last_mode(s):
        g_re, g_im = back(s, pm - 1)
        gp[s, 0] += g_re
        gp[s, 1] += g_im
        swap_grad(s).start()

    def put(s):
        swap_grad(s).wait_recv()
        drop, top, shift, base = corner_of(s)
        value = gp[s, m] + gr[s]
        x = pltpu.roll(jnp.concatenate([value, jnp.zeros((8, side), F32)], 0), drop, 0)
        x = jnp.concatenate([x, jnp.zeros((tall_rows, 128), F32)], 1)
        zbuf[rows - 8:rows + side, side:side + wide_cols] = pltpu.roll(x, shift, 1)

        @pl.loop(0, (rows + side) // 64)
        def _(i):
            at = pl.multiple_of(i * 64, 8)
            grad[pl.ds(at, 64), :] += zbuf[pl.ds((rows // 8 - 1 + i * 8 - top) * 8, 64),
                                           pl.ds((side // 128 - base) * 128, cols + side)]

    @pl.loop(0, cap)
    def _(s):
        last_mode(s)
    for q in early:
        first(q)
    for q in late:
        rs(q, 0).start()

    @pl.loop(0, cap)
    def _(s):
        put(s)

    def edge(i, src, dst, to):
        return remote(src, dst, es.at[i], er.at[i], to)
    quart = side // 4
    c_c = [edge(i, grad.at[rows + i * half:rows + (i + 1) * half, cols:cols + side],
                r_c.at[i * half:(i + 1) * half], down_dev) for i in range(2)]
    c_t = [edge(2 + i, grad.at[i * half:(i + 1) * half, cols:cols + side],
                r_r.at[i * half:(i + 1) * half], right_dev) for i in range(2)]
    span = (rows - side) // 2
    c_l = [edge(4 + i, grad.at[side + i * span:side + (i + 1) * span, cols:cols + side],
                r_r.at[side + i * span:side + (i + 1) * span], right_dev) for i in range(2)]
    c_b = [edge(6 + i, grad.at[rows + i * quart:rows + (i + 1) * quart, 0:cols],
                r_b.at[i * quart:(i + 1) * quart], down_dev) for i in range(4)]

    def send(copies, when):
        @pl.when(when)
        def _():
            for c in copies:
                c.start()

    def merge(i):
        @pl.when(right & (u > 0))
        def _():
            c_c[i].wait_recv()
            grad[i * half:(i + 1) * half, cols:cols + side] += r_c[i * half:(i + 1) * half]
        send([c_t[i]], right)

    send(c_c[:1], below & right)
    send(c_l[:1], right)
    send(c_c[1:], below & right)
    for q in early:
        second(q)
    send(c_l[1:], right)
    for q in late:
        first(q)
    send(c_b[:1], below)
    for q in early:
        z_sum(q)
    send(c_b[1:2], below)
    merge(0)
    for q in late:
        second(q)
    for q in early:
        gather(q)
    merge(1)
    send(c_b[2:3], below)
    send(c_b[3:], below)
    for q in late:
        z_sum(q)
    for q in early:
        spread(q)
    for q in late:
        gather(q)

    fin[...] = grad[0:rows, 0:cols]

    @pl.when(v > 0)
    def _():
        for c in c_l + c_t:
            c.wait_recv()
        fin[:, 0:side] += r_r[...]

    @pl.when(u > 0)
    def _():
        for c in c_b:
            c.wait_recv()
        fin[0:side, :] += r_b[...]

    hrow = rows // 2
    swap = remote(fin.at[pl.ds(pl.multiple_of(o * hrow, 8), hrow)], out.at[m], es.at[10], er.at[10], other)
    swap.start()
    out[m] = fin[pl.ds(pl.multiple_of(m * hrow, 8), hrow), :]
    for q in late:
        spread(q)
    swap.wait_recv()
    for q in (*early, *late):
        ag(q, 1).wait_recv()

    for n, (src, place, goes, comes, target) in enumerate(hops):
        @pl.when(goes)
        def _(n=n):
            outs[n].wait_send()

        @pl.when(comes)
        def _(n=n):
            fwds[n].wait_send()

    @pl.loop(0, cap)
    def _(s):
        swap_power(s).wait_send()
        swap_grad(s).wait_send()
    for q in (*early, *late):
        for c in (rs(q, 0), rs(q, 1), ag(q, 0), ag(q, 1)):
            c.wait_send()
        for d in range(1, ny):
            z_rs(q, d).wait_send()
            z_ag(q, d).wait_send()
    swap.wait_send()

    @pl.when(below)
    def _():
        for c in c_b:
            c.wait_send()

    @pl.when(right)
    def _():
        for c in c_l + c_t:
            c.wait_send()

    @pl.when(below & right)
    def _():
        for c in c_c:
            c.wait_send()


def local(nx, ny, object_field, probe, offsets, counts, amplitude):
    side = probe.shape[2]
    pm = probe.shape[1]
    rows, cols = object_field.shape[1:]
    cap = offsets.shape[2]
    dma = pltpu.SemaphoreType.DMA
    tall, wide, picks = tables(side)
    half = side // 2
    chunks = 2 if ny <= half // 16 else 1
    per = 4 + 2 * (ny - 1)
    slab = half // chunks
    cut = max(1, 8 * ny // slab)
    parts = pm * chunks
    assert nx == 4 and pm == 2

    def vm(*shape):
        return pltpu.VMEM(shape, F32)
    grad, pg = pl.pallas_call(
        functools.partial(fused_kernel, nx, ny, chunks),
        name="fused",
        out_shape=(jax.ShapeDtypeStruct((2, rows // 2, cols), F32), jax.ShapeDtypeStruct((2, pm, 2, half, side), F32)),
        in_specs=[SM, SM, ANY, ANY, ANY, ANY, ANY, ANY],
        out_specs=(VM, VM),
        scratch_shapes=[
            vm(2, rows + side, cols + side), vm(2, pm, side, side), vm(cap, side, side),
            pltpu.VMEM(tall.shape, BF16), pltpu.VMEM(wide.shape, BF16), pltpu.VMEM(picks.shape, BF16),
            vm(cap, 2, side, side), vm(cap, pm, 2, side, side), vm(cap, side, side), vm(cap, side, side),
            vm(cap, 2, side, side), vm(cap, side, side), vm(2 * (rows - 8) + side + 8, cols + 2 * side),
            vm(rows + side, cols + side),
            vm(2, pm, 2, half, side), vm(pm, 3, half, side), vm(parts, ny - 1, slab * cut // ny, side // cut),
            vm(rows, side), vm(side, cols), vm(side, side), vm(rows, cols),
            dma((6,)), dma((8,)), dma((8,)), dma((cap,)), dma((cap,)), dma((cap,)), dma((cap,)), dma((11,)), dma((11,)),
            dma((parts * per,)), dma((parts * per,)),
        ],
        compiler_params=pltpu.CompilerParams(collective_id=0, has_side_effects=True, vmem_limit_bytes=56 << 20),
    )(offsets[0, 0].T, counts[0], object_field, probe, amplitude,
      jnp.asarray(tall), jnp.asarray(wide), jnp.asarray(picks))
    return grad, pg.reshape(2, pm, side, side)


def solution(mesh):
    return jax.shard_map(
        functools.partial(local, mesh.shape["gx"], mesh.shape["gy"]),
        mesh=mesh,
        in_specs=(
            P(None, "gx", "gy"),
            P(None, "ma", None, None),
            P("gx", "gy", None, None),
            P("gx", "gy"),
            P("gx", "gy", None, None, None),
        ),
        out_specs=(P(None, ("gx", "ma"), "gy"), P(None, "ma", None, None)),
        check_vma=False,
    )
```

```python
import functools

import jax
import jax.numpy as jnp
import ml_dtypes
import numpy as np
from jax import lax
from jax.experimental import pallas as pl
from jax.experimental.pallas import tpu as pltpu
from jax.sharding import PartitionSpec as P

F32 = jnp.float32
BF16 = jnp.bfloat16
MESH = pl.DeviceIdType.MESH
ANY = pl.BlockSpec(memory_space=pl.ANY)
SM = pl.BlockSpec(memory_space=pltpu.SMEM)
VM = pl.BlockSpec(memory_space=pltpu.VMEM)


def tables(side):
    half = side // 2
    line = np.arange(half)
    found = []
    for odd in (0, 1):
        product = (2 * line[:, None] + odd) * line[None, :] % side
        value = np.exp(-2j * np.pi * product / side) / np.sqrt(side)
        block = np.block([[value.real, -value.imag], [value.imag, value.real]])
        found.append(block)

    def parts(block):
        high = block.astype(np.float32).astype(ml_dtypes.bfloat16)
        low = (block - high.astype(np.float64)).astype(np.float32).astype(ml_dtypes.bfloat16)
        return high, high, low

    tall = [np.concatenate(parts(b), 0) for b in (found[0].T, found[1].T, found[0], found[1])]
    wide = [np.concatenate(parts(b), 1) for b in (found[0], found[1], found[0].T, found[1].T)]
    order = np.concatenate([np.arange(0, side, 2), np.arange(1, side, 2)])
    pick = np.zeros((side, side), np.float32)
    pick[order, np.arange(side)] = 1.0
    picks = np.stack([pick, pick.T]).astype(ml_dtypes.bfloat16)
    return np.stack(tall), np.stack(wide), picks


def split(x):
    high = x.astype(BF16)
    return high, (x - high.astype(F32)).astype(BF16)


def right_mul(x, table):
    high, low = split(x)
    return jnp.dot(jnp.concatenate([high, low, high], 1), table, preferred_element_type=F32)


def left_mul(table, x):
    high, low = split(x)
    return jnp.dot(table, jnp.concatenate([high, low, high], 0), preferred_element_type=F32)


def remote(src, dst, send, recv, where):
    return pltpu.make_async_remote_copy(src_ref=src, dst_ref=dst, send_sem=send, recv_sem=recv,
                                        device_id=where, device_id_type=MESH)


def fused_kernel(nx, ny, chunks, off_ref, cnt_ref, obj, probe_hbm, amp_hbm, tall_hbm, wide_hbm, pick_hbm,
                 out, pout,
                 ext, probe, meas, tall, wide, pick, patch, far, pw, pwr, gp, gr, zbuf, grad,
                 acc, rg, rz, r_r, r_b, r_c, fin, lsem, hs, hr, ps, pr, gs, grs, es, er, as_, ar):
    u, v, m = lax.axis_index("gx"), lax.axis_index("gy"), lax.axis_index("ma")
    o = 1 - m
    side = probe.shape[2]
    half = side // 2
    pm = probe.shape[1]
    cap = meas.shape[0]
    rows, cols = obj.shape[1], obj.shape[2]
    other = (u, v, o)
    right, below = v < ny - 1, u < nx - 1
    left_dev, right_dev = (u, v - 1, m), (u, v + 1, m)
    up_dev, down_dev = (u - 1, v, m), (u + 1, v, m)

    local = [
        pltpu.make_async_copy(amp_hbm.at[0, 0], meas, lsem.at[0]),
        pltpu.make_async_copy(pick_hbm, pick, lsem.at[1]),
        pltpu.make_async_copy(obj, ext.at[:, 0:rows, 0:cols], lsem.at[2]),
        pltpu.make_async_copy(probe_hbm, probe, lsem.at[3]),
        pltpu.make_async_copy(tall_hbm, tall, lsem.at[4]),
        pltpu.make_async_copy(wide_hbm, wide, lsem.at[5]),
    ]
    for c in local:
        c.start()

    barrier = pltpu.get_barrier_semaphore()

    def greet(where):
        pl.semaphore_signal(barrier, inc=1, device_id=where, device_id_type=MESH)
    greet(other)
    for d in range(1, nx):
        greet((lax.rem(u + d, nx), v, m))
    for d in range(1, ny):
        greet((u, lax.rem(v + d, ny), m))

    @pl.when(jnp.logical_not(right))
    def _():
        ext[:, 0:rows, cols:cols + side] = jnp.zeros((2, rows, side), F32)

    @pl.when(jnp.logical_not(below))
    def _():
        ext[:, rows:rows + side, 0:cols] = jnp.zeros((2, side, cols), F32)

    @pl.when(jnp.logical_not(below & right))
    def _():
        ext[:, rows:rows + side, cols:cols + side] = jnp.zeros((2, side, side), F32)
    pl.semaphore_wait(barrier, nx + ny - 1)

    def piece(ref, r0, rn, c0, cn):
        return ref.at[m, r0:r0 + rn, c0:c0 + cn]

    h = rows - side
    first, rest = (0, side, cols, side), (side, h, cols, side)
    under, corner = (rows, side, 0, cols), (rows, side, cols, side)
    hops = [
        (piece(obj, 0, side, 0, side), first, v > 0, right, left_dev),
        (piece(obj, 0, side, 0, cols), under, u > 0, below, up_dev),
        (piece(obj, side, h, 0, side), rest, v > 0, right, left_dev),
        (piece(ext, *first), corner, (u > 0) & right, below & right, up_dev),
    ]
    outs, fwds = [], []
    for n, (src, place, goes, comes, target) in enumerate(hops):
        outs.append(remote(src, piece(ext, *place), hs.at[n], hr.at[n], target))
        fwds.append(remote(piece(ext, *place), piece(ext, *place), hs.at[4 + n], hr.at[4 + n], other))
    for n in range(3):
        @pl.when(hops[n][2])
        def _(n=n):
            outs[n].start()

    @pl.loop(0, zbuf.shape[0] // 8)
    def _(i):
        zbuf[pl.ds(pl.multiple_of(i * 8, 8), 8), :] = jnp.zeros((8, zbuf.shape[1]), F32)
    grad[...] = jnp.zeros_like(grad)
    acc[...] = jnp.zeros_like(acc)
    local[0].wait()
    local[1].wait()

    @pl.loop(0, cap)
    def _(s):
        measured = jnp.zeros((side, side), F32)
        for term in split(meas[s]):
            moved = jnp.dot(term, pick[0], preferred_element_type=F32).astype(BF16)
            measured = measured + jnp.dot(pick[1], moved, preferred_element_type=F32)
        meas[s] = measured

    for n, (src, place, goes, comes, target) in enumerate(hops):
        @pl.when(comes)
        def _(n=n):
            outs[n].wait_recv()
            if n == 0:
                @pl.when(u > 0)
                def _():
                    outs[3].start()
            fwds[n].start()
    for c in local[2:]:
        c.wait()
    for n, (src, place, goes, comes, target) in enumerate(hops):
        @pl.when(comes)
        def _(n=n):
            fwds[n].wait_recv()

    tall_rows, wide_cols = side + 8, side + 128

    def corner_of(s):
        row, col = off_ref[0, s], off_ref[1, s]
        return lax.rem(row, 8), lax.div(row, 8), lax.rem(col, 128), lax.div(col, 128)

    def swap_power(s):
        return remote(pw.at[s], pwr.at[s], ps.at[s], pr.at[s], other)

    @pl.loop(0, cap)
    def _(s):
        drop, top, shift, base = corner_of(s)

        def take(part):
            x = ext[part, pl.ds(top * 8, tall_rows), pl.ds(base * 128, wide_cols)]
            x = pltpu.roll(x, lax.rem(wide_cols - shift, wide_cols), 1)[:, :side]
            return pltpu.roll(x, lax.rem(tall_rows - drop, tall_rows), 0)[:side]

        a_re, a_im = take(0), take(1)
        patch[s, 0] = a_re
        patch[s, 1] = a_im
        pow_e = pow_o = jnp.zeros((half, side), F32)
        for k in range(pm):
            p_re, p_im = probe[0, k], probe[1, k]
            e_re = p_re * a_re - p_im * a_im
            e_im = p_re * a_im + p_im * a_re
            x_e = jnp.concatenate([e_re[:, :half] + e_re[:, half:], e_im[:, :half] + e_im[:, half:]], 1)
            x_o = jnp.concatenate([e_re[:, :half] - e_re[:, half:], e_im[:, :half] - e_im[:, half:]], 1)
            z_e = right_mul(x_e, tall[0])
            z_o = right_mul(x_o, tall[1])
            z_re = jnp.concatenate([z_e[:, :half], z_o[:, :half]], 1)
            z_im = jnp.concatenate([z_e[:, half:], z_o[:, half:]], 1)
            y_e = jnp.concatenate([z_re[:half] + z_re[half:], z_im[:half] + z_im[half:]], 0)
            y_o = jnp.concatenate([z_re[:half] - z_re[half:], z_im[:half] - z_im[half:]], 0)
            f_e = left_mul(wide[0], y_e)
            f_o = left_mul(wide[1], y_o)
            far[s, k, 0] = f_e
            far[s, k, 1] = f_o
            pow_e = pow_e + (f_e[:half] * f_e[:half] + f_e[half:] * f_e[half:])
            pow_o = pow_o + (f_o[:half] * f_o[:half] + f_o[half:] * f_o[half:])
        pw[s, :half] = pow_e
        pw[s, half:] = pow_o
        swap_power(s).start()

    def back(s, k):
        fac = meas[s]
        fac_e = jnp.concatenate([fac[:half], fac[:half]], 0)
        fac_o = jnp.concatenate([fac[half:], fac[half:]], 0)
        q_e = left_mul(wide[2], far[s, k, 0] * fac_e)
        q_o = left_mul(wide[3], far[s, k, 1] * fac_o)
        up, low = q_e + q_o, q_e - q_o
        w_re = jnp.concatenate([up[:half], low[:half]], 0)
        w_im = jnp.concatenate([up[half:], low[half:]], 0)
        s_e = right_mul(jnp.concatenate([w_re[:, :half], w_im[:, :half]], 1), tall[2])
        s_o = right_mul(jnp.concatenate([w_re[:, half:], w_im[:, half:]], 1), tall[3])
        fst, snd = s_e + s_o, s_e - s_o
        b_re = jnp.concatenate([fst[:, :half], snd[:, :half]], 1)
        b_im = jnp.concatenate([fst[:, half:], snd[:, half:]], 1)
        a_re, a_im = patch[s, 0], patch[s, 1]
        acc[0, k] += (a_re * b_re + a_im * b_im).reshape(2, half, side)
        acc[1, k] += (a_re * b_im - a_im * b_re).reshape(2, half, side)
        p_re, p_im = probe[0, k], probe[1, k]
        return p_re * b_re + p_im * b_im, p_re * b_im - p_im * b_re

    @pl.loop(0, cap)
    def _(s):
        swap_power(s).wait_recv()
        live = jnp.where(s < cnt_ref[0], 1.0, 0.0).astype(F32)
        meas[s] = live * (1.0 - meas[s] * lax.rsqrt(jnp.maximum(pw[s] + pwr[s], 0.25)))
        g_re, g_im = back(s, 0)
        gp[s, 0] = g_re
        gp[s, 1] = g_im

    slab = half // chunks
    hy, hx = u // 2, lax.rem(u, 2)
    by_y, by_x = (lax.rem(u + 2, 4), v, m), (u + 1 - 2 * hx, v, m)
    per = 4 + 2 * (ny - 1)
    cut = max(1, 8 * ny // slab)
    prow, pcol = slab * cut // ny, side // cut

    def across(q):
        return q // chunks, pl.ds(q % chunks * slab, slab)

    def x_leads(q):
        return q % 2 == 1 and chunks > 1

    def rs(q, n):
        k, c = across(q)
        if x_leads(q):
            src, to = (acc.at[:, k, 1 - hx, c], by_x) if n == 0 else (acc.at[1 - hy, k, hx, c], by_y)
        else:
            src, to = (acc.at[1 - hy, k, :, c], by_y) if n == 0 else (acc.at[hy, k, 1 - hx, c], by_x)
        return remote(src, rg.at[k, 0:2, c] if n == 0 else rg.at[k, 2, c],
                      as_.at[q * per + n], ar.at[q * per + n], to)

    def first(q):
        k, c = across(q)
        rs(q, 0).wait_recv()
        if x_leads(q):
            acc[:, k, hx, c] += rg[k, 0:2, c]
        else:
            acc[hy, k, :, c] += rg[k, 0:2, c]
        rs(q, 1).start()

    def zplace(ref, q, at):
        k = q // chunks
        r = q % chunks * slab + (at // cut) * prow
        c = lax.rem(at, cut) * pcol
        return ref.at[hy, k, hx, pl.ds(pl.multiple_of(r, 8), prow), pl.ds(pl.multiple_of(c, 128), pcol)]

    def z_rs(q, d):
        to = lax.rem(v + d, ny)
        i = q * per + 4 + d - 1
        return remote(zplace(acc, q, to), rz.at[q, d - 1], as_.at[i], ar.at[i], (u, to, m))

    def z_ag(q, d):
        to = lax.rem(v + d, ny)
        i = q * per + 4 + ny - 1 + d - 1
        at = zplace(pout, q, v)
        return remote(at, at, as_.at[i], ar.at[i], (u, to, m))

    def second(q):
        k, c = across(q)
        rs(q, 1).wait_recv()
        acc[hy, k, hx, c] += rg[k, 2, c]
        for d in range(1, ny):
            z_rs(q, d).start()

    def z_sum(q):
        total = zplace(acc, q, v)[...]
        for d in range(1, ny):
            z_rs(q, d).wait_recv()
            total = total + rz[q, d - 1]
        zplace(pout, q, v)[...] = total
        for d in range(1, ny):
            z_ag(q, d).start()

    def ag(q, n):
        k, c = across(q)
        x_first = q % 2 == 0
        if n == 0:
            at, to = pout.at[hy, k, hx, c], by_x if x_first else by_y
        elif x_first:
            at, to = pout.at[hy, k, :, c], by_y
        else:
            at, to = pout.at[:, k, hx, c], by_x
        return remote(at, at, as_.at[q * per + 2 + n], ar.at[q * per + 2 + n], to)

    def gather(q):
        for d in range(1, ny):
            z_ag(q, d).wait_recv()
        ag(q, 0).start()

    def spread(q):
        ag(q, 0).wait_recv()
        ag(q, 1).start()

    early, late = range(chunks), range(chunks, 2 * chunks)
    for q in early:
        rs(q, 0).start()

    def swap_grad(s):
        return remote(gp.at[s, o], gr.at[s], gs.at[s], grs.at[s], other)

    def last_mode(s):
        g_re, g_im = back(s, pm - 1)
        gp[s, 0] += g_re
        gp[s, 1] += g_im
        swap_grad(s).start()

    def put(s):
        swap_grad(s).wait_recv()
        drop, top, shift, base = corner_of(s)
        value = gp[s, m] + gr[s]
        x = pltpu.roll(jnp.concatenate([value, jnp.zeros((8, side), F32)], 0), drop, 0)
        x = jnp.concatenate([x, jnp.zeros((tall_rows, 128), F32)], 1)
        zbuf[rows - 8:rows + side, side:side + wide_cols] = pltpu.roll(x, shift, 1)

        @pl.loop(0, (rows + side) // 64)
        def _(i):
            at = pl.multiple_of(i * 64, 8)
            grad[pl.ds(at, 64), :] += zbuf[pl.ds((rows // 8 - 1 + i * 8 - top) * 8, 64),
                                           pl.ds((side // 128 - base) * 128, cols + side)]

    @pl.loop(0, cap)
    def _(s):
        last_mode(s)
    for q in early:
        first(q)
    for q in late:
        rs(q, 0).start()

    @pl.loop(0, cap)
    def _(s):
        put(s)

    def edge(i, src, dst, to):
        return remote(src, dst, es.at[i], er.at[i], to)
    quart = side // 4
    c_c = [edge(i, grad.at[rows + i * half:rows + (i + 1) * half, cols:cols + side],
                r_c.at[i * half:(i + 1) * half], down_dev) for i in range(2)]
    c_t = [edge(2 + i, grad.at[i * half:(i + 1) * half, cols:cols + side],
                r_r.at[i * half:(i + 1) * half], right_dev) for i in range(2)]
    span = (rows - side) // 2
    c_l = [edge(4 + i, grad.at[side + i * span:side + (i + 1) * span, cols:cols + side],
                r_r.at[side + i * span:side + (i + 1) * span], right_dev) for i in range(2)]
    c_b = [edge(6 + i, grad.at[rows + i * quart:rows + (i + 1) * quart, 0:cols],
                r_b.at[i * quart:(i + 1) * quart], down_dev) for i in range(4)]

    def send(copies, when):
        @pl.when(when)
        def _():
            for c in copies:
                c.start()

    def merge(i):
        @pl.when(right & (u > 0))
        def _():
            c_c[i].wait_recv()
            grad[i * half:(i + 1) * half, cols:cols + side] += r_c[i * half:(i + 1) * half]
        send([c_t[i]], right)

    send(c_c[:1], below & right)
    send(c_l[:1], right)
    send(c_c[1:], below & right)
    for q in early:
        second(q)
    send(c_l[1:], right)
    for q in late:
        first(q)
    send(c_b[:1], below)
    for q in early:
        z_sum(q)
    send(c_b[1:2], below)
    merge(0)
    for q in late:
        second(q)
    for q in early:
        gather(q)
    merge(1)
    send(c_b[2:3], below)
    send(c_b[3:], below)
    for q in late:
        z_sum(q)
    for q in early:
        spread(q)
    for q in late:
        gather(q)

    fin[...] = grad[0:rows, 0:cols]

    @pl.when(v > 0)
    def _():
        for c in c_l + c_t:
            c.wait_recv()
        fin[:, 0:side] += r_r[...]

    @pl.when(u > 0)
    def _():
        for c in c_b:
            c.wait_recv()
        fin[0:side, :] += r_b[...]

    hrow = rows // 2
    swap = remote(fin.at[pl.ds(pl.multiple_of(o * hrow, 8), hrow)], out.at[m], es.at[10], er.at[10], other)
    swap.start()
    out[m] = fin[pl.ds(pl.multiple_of(m * hrow, 8), hrow), :]
    for q in late:
        spread(q)
    swap.wait_recv()
    for q in (*early, *late):
        ag(q, 1).wait_recv()

    for n, (src, place, goes, comes, target) in enumerate(hops):
        @pl.when(goes)
        def _(n=n):
            outs[n].wait_send()

        @pl.when(comes)
        def _(n=n):
            fwds[n].wait_send()

    @pl.loop(0, cap)
    def _(s):
        swap_power(s).wait_send()
        swap_grad(s).wait_send()
    for q in (*early, *late):
        for c in (rs(q, 0), rs(q, 1), ag(q, 0), ag(q, 1)):
            c.wait_send()
        for d in range(1, ny):
            z_rs(q, d).wait_send()
            z_ag(q, d).wait_send()
    swap.wait_send()

    @pl.when(below)
    def _():
        for c in c_b:
            c.wait_send()

    @pl.when(right)
    def _():
        for c in c_l + c_t:
            c.wait_send()

    @pl.when(below & right)
    def _():
        for c in c_c:
            c.wait_send()


def local(nx, ny, object_field, probe, offsets, counts, amplitude):
    side = probe.shape[2]
    pm = probe.shape[1]
    rows, cols = object_field.shape[1:]
    cap = offsets.shape[2]
    dma = pltpu.SemaphoreType.DMA
    tall, wide, picks = tables(side)
    half = side // 2
    chunks = 4 if ny <= half // 32 else 1
    per = 4 + 2 * (ny - 1)
    slab = half // chunks
    cut = max(1, 8 * ny // slab)
    parts = pm * chunks
    assert nx == 4 and pm == 2

    def vm(*shape):
        return pltpu.VMEM(shape, F32)
    grad, pg = pl.pallas_call(
        functools.partial(fused_kernel, nx, ny, chunks),
        name="fused",
        out_shape=(jax.ShapeDtypeStruct((2, rows // 2, cols), F32), jax.ShapeDtypeStruct((2, pm, 2, half, side), F32)),
        in_specs=[SM, SM, ANY, ANY, ANY, ANY, ANY, ANY],
        out_specs=(VM, VM),
        scratch_shapes=[
            vm(2, rows + side, cols + side), vm(2, pm, side, side), vm(cap, side, side),
            pltpu.VMEM(tall.shape, BF16), pltpu.VMEM(wide.shape, BF16), pltpu.VMEM(picks.shape, BF16),
            vm(cap, 2, side, side), vm(cap, pm, 2, side, side), vm(cap, side, side), vm(cap, side, side),
            vm(cap, 2, side, side), vm(cap, side, side), vm(2 * (rows - 8) + side + 8, cols + 2 * side),
            vm(rows + side, cols + side),
            vm(2, pm, 2, half, side), vm(pm, 3, half, side), vm(parts, ny - 1, slab * cut // ny, side // cut),
            vm(rows, side), vm(side, cols), vm(side, side), vm(rows, cols),
            dma((6,)), dma((8,)), dma((8,)), dma((cap,)), dma((cap,)), dma((cap,)), dma((cap,)), dma((11,)), dma((11,)),
            dma((parts * per,)), dma((parts * per,)),
        ],
        compiler_params=pltpu.CompilerParams(collective_id=0, has_side_effects=True, vmem_limit_bytes=56 << 20),
    )(offsets[0, 0].T, counts[0], object_field, probe, amplitude,
      jnp.asarray(tall), jnp.asarray(wide), jnp.asarray(picks))
    return grad, pg.reshape(2, pm, side, side)


def solution(mesh):
    return jax.shard_map(
        functools.partial(local, mesh.shape["gx"], mesh.shape["gy"]),
        mesh=mesh,
        in_specs=(
            P(None, "gx", "gy"),
            P(None, "ma", None, None),
            P("gx", "gy", None, None),
            P("gx", "gy"),
            P("gx", "gy", None, None, None),
        ),
        out_specs=(P(None, ("gx", "ma"), "gy"), P(None, "ma", None, None)),
        check_vma=False,
    )
```
